128 devices in a mesh: row: 8 (over z_hi, y), col: 16 (over z_lo, x, core).
Axes of the slice: x: 4, y: 4, z: 4 (z_hi: 2, z_lo: 2; z = z_hi * 2 + z_lo), core: 2. Of those that a mesh axis runs over, the one named last changes fastest.
Arguments:
- gram: float32 [8192, 8192], P('row', 'col'), may hold values from -6 to 8
- rotations: float32 [2, 8, 1024, 1024], P(None, 'row', 'col'), may hold values from -1 to 2
Outputs:
- rotated: float32 [8192, 8192], P('row', 'col')
The draws below stay inside these ranges and needn't reach their ends.
All inputs are finite; a program needn't handle non-finite values.
Results may differ from the reference program's by a relative error of at most 0.00016.
Values sent between devices are 32-bit elements; how exact they have to be, the bound alone decides.
No kernel may reach another device: no remote copies, remote signals or barrier semaphores. Data moves between devices by JAX's collectives and lax.ppermute only.
A program may use at most 64 MiB of HBM per device.

```python
import jax
import jax.numpy as jnp
import numpy as np
from jax import lax

BLOCK = 512
STEPS = 2
PAIRS = 8
ORDER = 8192


def draw_gram(key, part):
    first = jax.random.fold_in(key, 0)
    base = jnp.clip(jax.random.normal(first, (ORDER, ORDER), jnp.float32), -5.0, 5.0)
    sym = 0.5 * (base + base.T)
    return sym + 2.0 * jnp.eye(ORDER, dtype=jnp.float32)


def draw_rotations(key, part):
    size = 2 * BLOCK
    sigma = 0.5 / size ** 0.5
    shape = (STEPS, PAIRS, size, size)
    noise = jnp.clip(jax.random.normal(key, shape, jnp.float32), -6.0, 6.0) * sigma
    return noise + jnp.eye(size, dtype=jnp.float32)


def setup_inputs(seed: int = 0) -> dict:
    splits = jax.random.split(jax.random.key(seed), 3)
    return {
        "gram": draw_gram(jax.random.fold_in(splits[2], 71), 0),
        "rotations": draw_rotations(jax.random.fold_in(splits[2], 71), 0),
    }


def move_order(pair_count):
    order = np.zeros(2 * pair_count, dtype=np.int32)
    for pair in range(pair_count):
        if pair == 0:
            order[0] = 0
        elif pair == 1:
            order[2] = 1
        else:
            order[2 * pair] = 2 * pair - 2
        if pair < pair_count - 1:
            order[2 * pair + 1] = 2 * pair + 3
        else:
            order[2 * pair + 1] = 2 * pair
    return order


def reference(gram, rotations):
    pair_count = PAIRS
    blocks = 2 * pair_count
    order = jnp.asarray(move_order(pair_count))
    current = gram
    for step in range(STEPS):
        turn = rotations[step].astype(jnp.float32)
        cols = current.reshape(ORDER, pair_count, 2 * BLOCK)
        cols = jnp.einsum("npa,pab->npb", cols, turn, precision=lax.Precision.HIGHEST)
        current = cols.reshape(ORDER, ORDER)
        rows = current.reshape(pair_count, 2 * BLOCK, ORDER)
        rows = jnp.einsum("pab,pan->pbn", turn, rows, precision=lax.Precision.HIGHEST)
        tiles = rows.reshape(blocks, BLOCK, blocks, BLOCK)
        tiles = jnp.take(tiles, order, axis=0)
        tiles = jnp.take(tiles, order, axis=2)
        current = tiles.reshape(ORDER, ORDER)
    return current
```

```python
import jax
import jax.numpy as jnp
from jax import lax
from jax.sharding import PartitionSpec as P

HIGH = lax.Precision.HIGH


def place(index):
    row, col = divmod(index, 16)
    return (row // 4, row % 4, col // 8, (col // 2) % 4, col % 2)


def index_of(z_hi, y, z_lo, x, core):
    return (z_hi * 4 + y % 4) * 16 + z_lo * 8 + (x % 4) * 2 + core


def pairs_of(move):
    return [(i, index_of(*move(*place(i)))) for i in range(128)]


def along_x(step):
    return pairs_of(lambda zh, y, zl, x, c: (zh, y, zl, x + step, c))


def along_y(step):
    return pairs_of(lambda zh, y, zl, x, c: (zh, y + step, zl, x, c))


NEXT_X, PREV_X = along_x(1), along_x(-1)
NEXT_Y, PREV_Y = along_y(1), along_y(-1)
OTHER_LO = pairs_of(lambda zh, y, zl, x, c: (zh, y, 1 - zl, x, c))
OTHER_HI = pairs_of(lambda zh, y, zl, x, c: (1 - zh, y, zl, x, c))
OTHER_CORE = pairs_of(lambda zh, y, zl, x, c: (zh, y, zl, x, 1 - c))
TRANSPOSE = pairs_of(lambda zh, y, zl, x, c: (zl, x, zh, y, c))


def new_position(old):
    if old == 0:
        return 0
    if old == 1:
        return 2
    if old == 14:
        return 15
    return old + 2 if old % 2 == 0 else old - 2


MOVE_COL = [(r * 16 + c, r * 16 + new_position(c)) for r in range(8) for c in range(16)]
ROW_UP = [(r * 16 + c, (r + 1) * 16 + c) for r in range(7) for c in range(16)]
ROW_DOWN = [(r * 16 + c, (r - 1) * 16 + c) for r in range(1, 8) for c in range(16)]


def send(value, pairs):
    return lax.ppermute(value, ("row", "col"), pairs)


def ring_gather(own, other, forward, backward, ring, plane):
    half = own.shape[0] // 2
    across = send(own, other)
    before = send(own, forward)
    after = send(own, backward)
    ahead = send(jnp.concatenate([across, before[:half]]), forward)
    behind = send(jnp.concatenate([across, after[half:]]), backward)
    across_before, opposite_1 = ahead[: 2 * half], ahead[2 * half :]
    across_after, opposite_2 = behind[: 2 * half], behind[2 * half :]
    far_1 = send(across_before[:half], forward)
    far_2 = send(across_after[half:], backward)
    opposite = jnp.concatenate([opposite_1, opposite_2])
    far = jnp.concatenate([far_1, far_2])
    out = jnp.zeros((8,) + own.shape, own.dtype)
    lines = [(plane, [own, after, opposite, before]), (1 - plane, [across, across_after, far, across_before])]
    for where, line in lines:
        for distance, piece in enumerate(line):
            at = where * 4 + (ring + distance) % 4
            out = lax.dynamic_update_slice(out, piece[None], (at, 0, 0))
    return out


def shards(gram, rotations):
    row_index = lax.axis_index("row")
    col_index = lax.axis_index("col")
    core = col_index % 2
    x = (col_index // 2) % 4
    z_lo = col_index // 8
    y = row_index % 4
    z_hi = row_index // 4
    n = 512

    def gather_row(piece):
        half = ring_gather(piece, OTHER_LO, NEXT_X, PREV_X, x, z_lo)
        other = send(half, OTHER_CORE)
        first = jnp.where(core == 0, half, other)
        second = jnp.where(core == 0, other, half)
        return jnp.stack([first, second], axis=1).reshape(2 * n, 2 * n)

    def gather_col(piece):
        mine = lax.dynamic_slice_in_dim(piece, core * n, n, 1)
        give = lax.dynamic_slice_in_dim(piece, (1 - core) * n, n, 1)
        got = send(give, OTHER_CORE)
        first = jnp.where(core == 0, mine, got)
        second = jnp.where(core == 0, got, mine)
        piece = send(jnp.concatenate([first, second]), TRANSPOSE)
        whole = ring_gather(piece, OTHER_HI, NEXT_Y, PREV_Y, y, z_hi)
        return whole.reshape(2 * n, n)

    def mix(turn, tile):
        return lax.dot_general(
            turn, tile, (((0,), (0,)), ((), ())), precision=HIGH, preferred_element_type=jnp.float32
        )

    def times(tile, turn):
        return jnp.dot(tile, turn, precision=HIGH, preferred_element_type=jnp.float32)

    def move(upper, lower):
        h = n // 2
        send_up = jnp.where(row_index == 0, lower, upper)
        sent = send(jnp.concatenate([upper[:h], lower[:h]]), MOVE_COL)
        up_2 = send(send_up[h:], ROW_UP)
        down_2 = send(lower[h:], ROW_DOWN)
        up_1 = send(jnp.where(row_index == 0, sent[h:], sent[:h]), ROW_UP)
        down_1 = send(sent[h:], ROW_DOWN)
        up_2 = jnp.where(row_index == 0, upper[h:], up_2)
        down_2 = jnp.where(row_index == 7, upper[h:], down_2)
        sent_2 = send(jnp.concatenate([up_2, down_2]), MOVE_COL)
        up_1 = jnp.where(row_index == 0, sent[:h], up_1)
        down_1 = jnp.where(row_index == 7, sent[:h], down_1)
        return jnp.concatenate([up_1, sent_2[:h], down_1, sent_2[h:]])

    row_turns = [gather_row(rotations[s, 0]) for s in range(2)]
    col_turns = [gather_col(rotations[s, 0]) for s in range(2)]
    current = gram
    for s in range(2):
        row_turn, col_turn = row_turns[s], col_turns[s]
        mixed = mix(row_turn, current)
        halves = []
        for part in (mixed[:n], mixed[n:]):
            other = send(part, OTHER_CORE)
            first = jnp.where(core == 0, part, other)
            second = jnp.where(core == 0, other, part)
            halves.append(times(first, col_turn[:n]) + times(second, col_turn[n:]))
        current = move(*halves)
    return current


def solution(mesh):
    placed = (P("row", "col"), P(None, "row", "col", None))
    return jax.shard_map(
        shards, mesh=mesh, in_specs=placed, out_specs=P("row", "col"), check_vma=False
    )
```

```python
import jax
import jax.numpy as jnp
from jax import lax
from jax.experimental import pallas as pl
from jax.experimental.pallas import tpu as pltpu
from jax.sharding import PartitionSpec as P


N = 512
F32 = jnp.float32
HIGH = lax.Precision.HIGH


def place(index):
    row, col = divmod(index, 16)
    return (row // 4, row % 4, col // 8, (col // 2) % 4, col % 2)


def index_of(z_hi, y, z_lo, x, core):
    return (z_hi * 4 + y % 4) * 16 + z_lo * 8 + (x % 4) * 2 + core


def pairs_of(move):
    return [(i, index_of(*move(*place(i)))) for i in range(128)]


def along_x(step):
    return pairs_of(lambda zh, y, zl, x, c: (zh, y, zl, x + step, c))


def along_y(step):
    return pairs_of(lambda zh, y, zl, x, c: (zh, y + step, zl, x, c))


OTHER_LO = pairs_of(lambda zh, y, zl, x, c: (zh, y, 1 - zl, x, c))
OTHER_HI = pairs_of(lambda zh, y, zl, x, c: (1 - zh, y, zl, x, c))
OTHER_CORE = pairs_of(lambda zh, y, zl, x, c: (zh, y, zl, x, 1 - c))
TRANSPOSE = pairs_of(lambda zh, y, zl, x, c: (zl, x, zh, y, c))


def new_position(old):
    if old == 0:
        return 0
    if old == 1:
        return 2
    if old == 14:
        return 15
    return old + 2 if old % 2 == 0 else old - 2


def moves(rises):
    out = []
    for r in range(8):
        for c in range(16):
            to = r + 1 if rises(c) else r - 1
            if 0 <= to < 8:
                out.append((r * 16 + c, to * 16 + new_position(c)))
    return out


MOVE_FIRST = moves(lambda c: c % 2 == 0)
MOVE_SECOND = moves(lambda c: c % 2 == 1)
MOVE_END = [(r * 16 + c, r * 16 + new_position(c)) for r in (0, 7) for c in range(16)]


def send(value, pairs):
    return lax.ppermute(value, ("row", "col"), pairs)


def vmem_call(body, inputs, outs):
    return pl.pallas_call(
        body,
        out_shape=[jax.ShapeDtypeStruct(shape, F32) for shape in outs],
        in_specs=[pl.BlockSpec(memory_space=pltpu.VMEM)] * len(inputs),
        out_specs=[pl.BlockSpec(memory_space=pltpu.VMEM)] * len(outs),
        compiler_params=pltpu.CompilerParams(vmem_limit_bytes=24 * 2**20),
        cost_estimate=pl.CostEstimate(flops=0, bytes_accessed=2**22, transcendentals=0),
    )(*inputs)


def rows_body(*refs):
    pieces, outs = refs[:8], refs[8:]
    col = lax.axis_index("col")
    ring, plane = (col // 2) % 4, col // 8
    for j in range(8):
        at = (plane if j < 4 else 1 - plane) * 4 + (ring + j % 4) % 4
        for half in range(2):
            first = at * 128 + 64 * jnp.where(col % 2 == 0, half, 1 - half)
            rows = pl.ds(pl.multiple_of(first, 64), 64)
            for step, out in enumerate(outs):
                out[rows, :] = pieces[j][step, half]


def join_body(own, other, out):
    own_first = lax.axis_index("row") != 0

    @pl.when(own_first)
    def _():
        out[:, 0:N] = own[...]
        out[:, N:] = other[...]

    @pl.when(jnp.logical_not(own_first))
    def _():
        out[:, 0:N] = other[...]
        out[:, N:] = own[...]


def cols_body(*refs):
    pieces, own, other = refs[:8], refs[8::2], refs[9::2]
    row, core = lax.axis_index("row"), lax.axis_index("col") % 2
    ring, plane = row % 4, row // 4

    def fill(first, second):
        for j in range(8):
            for half in range(2):
                at = (ring + j % 4) % 4 * 128 + 64 * jnp.where(core == 0, half, 1 - half)
                rows = pl.ds(pl.multiple_of(at, 64), 64)
                for step, out in enumerate(first if j < 4 else second):
                    out[rows, :] = pieces[j][step, half]

    @pl.when(plane == core)
    def _():
        fill(own, other)

    @pl.when(plane != core)
    def _():
        fill(other, own)


def mix(turn, tile):
    dims = (((0,), (0,)), ((), ()))
    return lax.dot_general(turn, tile, dims, precision=HIGH, preferred_element_type=F32)


def times(tile, turn):
    return jnp.dot(tile, turn, precision=HIGH, preferred_element_type=F32)


ROW_RING = (along_x(1), along_x(-1), along_x(2), OTHER_LO)
COL_RING = (along_y(1), along_y(-1), along_y(2), OTHER_HI)


def gather(own, ring):
    forward, backward, opposite, other = ring
    to = lambda value, pairs: send(value, pairs)
    across = to(own, other)
    before = to(own, forward)
    behind = to(own, backward)
    far = to(own, opposite)
    across_before = to(across, forward)
    across_behind = to(across, backward)
    across_far = to(far, other)
    return [own, behind, far, before, across, across_behind, across_far, across_before]


def shards(gram, rotations):
    row, col = lax.axis_index("row"), lax.axis_index("col")
    core = col % 2
    keep = lax.dynamic_slice_in_dim(rotations[:, 0], core * N, N, 2)
    give = lax.dynamic_slice_in_dim(rotations[:, 0], (1 - core) * N, N, 2)
    got = send(give, OTHER_CORE)
    piece = jnp.stack([keep, got], axis=1)
    turned = send(piece, TRANSPOSE)
    halves = vmem_call(rows_body, gather(piece, ROW_RING), [(2 * N, N)] * 2)
    cols = vmem_call(cols_body, gather(turned, COL_RING), [(N, N)] * 4)
    from_even = ((core == 0) & (col != 2)) | (col == 15)

    tile = gram
    for step in range(2):
        other = send(halves[step], OTHER_CORE)
        (turn,) = vmem_call(join_body, (halves[step], other), [(2 * N, 2 * N)])
        own_cols, other_cols = cols[2 * step : 2 * step + 2]
        mixed = mix(turn, tile)
        other = send(mixed, OTHER_CORE)
        parts = times(mixed[:N], own_cols), times(mixed[N:], own_cols)
        first, second = lax.optimization_barrier(parts)
        first = first + times(other[N:], other_cols)
        second = second + times(other[:N], other_cols)
        first, second = lax.optimization_barrier((first, second))
        ends = jnp.where((row == 7) == (core == 0), first, second)
        first = send(first, MOVE_FIRST)
        second = send(second, MOVE_SECOND)
        ends = send(ends, MOVE_END)
        upper = jnp.where(row == 0, ends, jnp.where(from_even, first, second))
        lower = jnp.where(row == 7, ends, jnp.where(from_even, second, first))
        tile = jnp.concatenate([upper, lower])
    return tile


def solution(mesh):
    placed = (P("row", "col"), P(None, "row", "col", None))
    return jax.shard_map(
        shards, mesh=mesh, in_specs=placed, out_specs=P("row", "col"), check_vma=False
    )
```

```python
import jax
import jax.numpy as jnp
from jax import lax
from jax.experimental import pallas as pl
from jax.experimental.pallas import tpu as pltpu
from jax.sharding import PartitionSpec as P


N = 512
F32 = jnp.float32
HIGH = lax.Precision.HIGH


def place(index):
    row, col = divmod(index, 16)
    return (row // 4, row % 4, col // 8, (col // 2) % 4, col % 2)


def index_of(z_hi, y, z_lo, x, core):
    return (z_hi * 4 + y % 4) * 16 + z_lo * 8 + (x % 4) * 2 + core


def pairs_of(move):
    return [(i, index_of(*move(*place(i)))) for i in range(128)]


def along_x(step):
    return pairs_of(lambda zh, y, zl, x, c: (zh, y, zl, x + step, c))


def along_y(step):
    return pairs_of(lambda zh, y, zl, x, c: (zh, y + step, zl, x, c))


OTHER_LO = pairs_of(lambda zh, y, zl, x, c: (zh, y, 1 - zl, x, c))
OTHER_HI = pairs_of(lambda zh, y, zl, x, c: (1 - zh, y, zl, x, c))
OTHER_CORE = pairs_of(lambda zh, y, zl, x, c: (zh, y, zl, x, 1 - c))
TRANSPOSE = pairs_of(lambda zh, y, zl, x, c: (zl, x, zh, y, c))


def new_position(old):
    if old == 0:
        return 0
    if old == 1:
        return 2
    if old == 14:
        return 15
    return old + 2 if old % 2 == 0 else old - 2


MOVE_COL = [(r * 16 + c, r * 16 + new_position(c)) for r in range(8) for c in range(16)]
ROW_UP = [(r * 16 + c, (r + 1) * 16 + c) for r in range(7) for c in range(16)]
ROW_DOWN = [(r * 16 + c, (r - 1) * 16 + c) for r in range(1, 8) for c in range(16)]


def send(value, pairs):
    return lax.ppermute(value, ("row", "col"), pairs)


def vmem_call(body, inputs, outs):
    return pl.pallas_call(
        body,
        out_shape=[jax.ShapeDtypeStruct(shape, F32) for shape in outs],
        in_specs=[pl.BlockSpec(memory_space=pltpu.VMEM)] * len(inputs),
        out_specs=[pl.BlockSpec(memory_space=pltpu.VMEM)] * len(outs),
        compiler_params=pltpu.CompilerParams(vmem_limit_bytes=12 * 2**20),
        cost_estimate=pl.CostEstimate(flops=0, bytes_accessed=2**22, transcendentals=0),
    )(*inputs)


def rows_body(*refs):
    pieces, out = refs[:8], refs[8]
    col = lax.axis_index("col")
    ring, plane = (col // 2) % 4, col // 8
    for j in range(8):
        at = (plane if j < 4 else 1 - plane) * 4 + (ring + j % 4) % 4
        for half in range(2):
            first = at * 128 + 64 * jnp.where(col % 2 == 0, half, 1 - half)
            rows = pl.ds(pl.multiple_of(first, 64), 64)
            out[rows, :] = pieces[j][half * 64 : half * 64 + 64, :]


def join_body(own, other, out):
    up_is_own = (lax.axis_index("col") % 2 == 0) != (lax.axis_index("row") == 0)

    @pl.when(up_is_own)
    def _():
        out[:, 0:N] = own[...]
        out[:, N:] = other[...]

    @pl.when(jnp.logical_not(up_is_own))
    def _():
        out[:, 0:N] = other[...]
        out[:, N:] = own[...]


def cols_body(*refs):
    pieces, own, other = refs[:8], refs[8], refs[9]
    row, core = lax.axis_index("row"), lax.axis_index("col") % 2
    ring, plane = row % 4, row // 4

    def fill(first, second):
        for j in range(8):
            out = first if j < 4 else second
            for part in range(2):
                at = (ring + j % 4) % 4 * 128 + 64 * jnp.where(core == 0, part, 1 - part)
                rows = pl.ds(pl.multiple_of(at, 64), 64)
                out[rows, :] = pieces[j][part * 64 : part * 64 + 64, :]

    @pl.when(plane == core)
    def _():
        fill(own, other)

    @pl.when(plane != core)
    def _():
        fill(other, own)


def mix(turn, tile):
    dims = (((0,), (0,)), ((), ()))
    return lax.dot_general(turn, tile, dims, precision=HIGH, preferred_element_type=F32)


def times(tile, turn):
    return jnp.dot(tile, turn, precision=HIGH, preferred_element_type=F32)


ROW_RING = (along_x(1), along_x(-1), along_x(2), OTHER_LO)
COL_RING = (along_y(1), along_y(-1), along_y(2), OTHER_HI)


def gather(own, ring):
    forward, backward, opposite, other = ring
    to = lambda value, pairs: send(value, pairs)
    across = to(own, other)
    before = to(own, forward)
    behind = to(own, backward)
    far = to(own, opposite)
    across_before = to(across, forward)
    across_behind = to(across, backward)
    across_far = to(far, other)
    return [own, behind, far, before, across, across_behind, across_far, across_before]


def shards(gram, rotations):
    row = lax.axis_index("row")
    core = lax.axis_index("col") % 2
    keep = lax.dynamic_slice_in_dim(rotations[:, 0], core * N, N, 2)
    give = lax.dynamic_slice_in_dim(rotations[:, 0], (1 - core) * N, N, 2)
    got = send(give, OTHER_CORE)

    def turns(step):
        at = int(step) - 1
        piece = jnp.concatenate([keep[at], got[at]])
        turned = send(piece, TRANSPOSE)
        (half,) = vmem_call(rows_body, gather(piece, ROW_RING), [(2 * N, N)])
        other = send(half, OTHER_CORE)
        (whole,) = vmem_call(join_body, (half, other), [(2 * N, 2 * N)])
        pieces = gather(turned, COL_RING)
        return whole, vmem_call(cols_body, pieces, [(N, N)] * 2)

    def advance(tile, rows, cols):
        own_cols, other_cols = cols
        mixed = mix(rows, tile)
        other = send(mixed, OTHER_CORE)
        own_parts = times(mixed[:N], own_cols), times(mixed[N:], own_cols)
        up, down = lax.optimization_barrier(own_parts)
        up = up + times(other[:N], other_cols)
        down = down + times(other[N:], other_cols)
        up = send(up, MOVE_COL)
        down = send(down, MOVE_COL)
        from_above = send(up, ROW_UP)
        from_below = send(down, ROW_DOWN)
        first = jnp.where(row == 0, down, from_above)
        second = jnp.where(row == 7, up, from_below)
        return jnp.concatenate([first, second])

    tile = gram
    for step in ("1", "2"):
        tile = advance(tile, *turns(step))
    return tile


def solution(mesh):
    placed = (P("row", "col"), P(None, "row", "col", None))
    return jax.shard_map(
        shards, mesh=mesh, in_specs=placed, out_specs=P("row", "col"), check_vma=False
    )
```

```python
import jax
import jax.numpy as jnp
from jax import lax
from jax.experimental import pallas as pl
from jax.experimental.pallas import tpu as pltpu
from jax.sharding import PartitionSpec as P


N = 512
F32 = jnp.float32
HIGH = lax.Precision.HIGH


def place(index):
    row, col = divmod(index, 16)
    return (row // 4, row % 4, col // 8, (col // 2) % 4, col % 2)


def index_of(z_hi, y, z_lo, x, core):
    return (z_hi * 4 + y % 4) * 16 + z_lo * 8 + (x % 4) * 2 + core


def pairs_of(move):
    return [(i, index_of(*move(*place(i)))) for i in range(128)]


def along_x(step):
    return pairs_of(lambda zh, y, zl, x, c: (zh, y, zl, x + step, c))


def along_y(step):
    return pairs_of(lambda zh, y, zl, x, c: (zh, y + step, zl, x, c))


OTHER_LO = pairs_of(lambda zh, y, zl, x, c: (zh, y, 1 - zl, x, c))
OTHER_HI = pairs_of(lambda zh, y, zl, x, c: (1 - zh, y, zl, x, c))
OTHER_CORE = pairs_of(lambda zh, y, zl, x, c: (zh, y, zl, x, 1 - c))
TRANSPOSE = pairs_of(lambda zh, y, zl, x, c: (zl, x, zh, y, c))


def new_position(old):
    if old == 0:
        return 0
    if old == 1:
        return 2
    if old == 14:
        return 15
    return old + 2 if old % 2 == 0 else old - 2


RELAYED = {(3, 0): (4, 8), (4, 0): (3, 8), (3, 14): (4, 6), (4, 14): (3, 6)}


def moves(rises):
    out = []
    for r in range(8):
        for c in range(16):
            to = r + 1 if rises(c) else r - 1
            relayed = (r, c) in RELAYED and {r, to} == {3, 4}
            if 0 <= to < 8 and not relayed:
                out.append((r * 16 + c, to * 16 + new_position(c)))
    return out


MOVE_FIRST = moves(lambda c: c % 2 == 0)
MOVE_SECOND = moves(lambda c: c % 2 == 1)
MOVE_END = [(r * 16 + c, r * 16 + new_position(c)) for r in (0, 7) for c in range(16)]
MOVE_END += [(r * 16 + c, to[0] * 16 + to[1]) for (r, c), to in RELAYED.items()]
FROM_RELAY = [(to[0] * 16 + to[1], to[0] * 16 + new_position(c)) for (_, c), to in RELAYED.items()]


def send(value, pairs):
    return lax.ppermute(value, ("row", "col"), pairs)


def vmem_call(body, inputs, outs):
    return pl.pallas_call(
        body,
        out_shape=[jax.ShapeDtypeStruct(shape, F32) for shape in outs],
        in_specs=[pl.BlockSpec(memory_space=pltpu.VMEM)] * len(inputs),
        out_specs=[pl.BlockSpec(memory_space=pltpu.VMEM)] * len(outs),
        compiler_params=pltpu.CompilerParams(vmem_limit_bytes=12 * 2**20),
        cost_estimate=pl.CostEstimate(flops=0, bytes_accessed=2**22, transcendentals=0),
    )(*inputs)


def rows_body(*refs):
    pieces, out = refs[:8], refs[8]
    col = lax.axis_index("col")
    ring, plane = (col // 2) % 4, col // 8
    for j in range(8):
        at = (plane if j < 4 else 1 - plane) * 4 + (ring + j % 4) % 4
        for half in range(2):
            first = at * 128 + 64 * jnp.where(col % 2 == 0, half, 1 - half)
            rows = pl.ds(pl.multiple_of(first, 64), 64)
            out[rows, :] = pieces[j][half * 64 : half * 64 + 64, :]


def join_body(own, other, out):
    own_first = lax.axis_index("row") != 0

    @pl.when(own_first)
    def _():
        out[:, 0:N] = own[...]
        out[:, N:] = other[...]

    @pl.when(jnp.logical_not(own_first))
    def _():
        out[:, 0:N] = other[...]
        out[:, N:] = own[...]


def cols_body(*refs):
    pieces, own, other = refs[:8], refs[8], refs[9]
    row, core = lax.axis_index("row"), lax.axis_index("col") % 2
    ring, plane = row % 4, row // 4

    def fill(first, second):
        for j in range(8):
            out = first if j < 4 else second
            for part in range(2):
                at = (ring + j % 4) % 4 * 128 + 64 * jnp.where(core == 0, part, 1 - part)
                rows = pl.ds(pl.multiple_of(at, 64), 64)
                out[rows, :] = pieces[j][part * 64 : part * 64 + 64, :]

    @pl.when(plane == core)
    def _():
        fill(own, other)

    @pl.when(plane != core)
    def _():
        fill(other, own)


def mix(turn, tile):
    dims = (((0,), (0,)), ((), ()))
    return lax.dot_general(turn, tile, dims, precision=HIGH, preferred_element_type=F32)


def times(tile, turn):
    return jnp.dot(tile, turn, precision=HIGH, preferred_element_type=F32)


ROW_RING = (along_x(1), along_x(-1), along_x(2), OTHER_LO)
COL_RING = (along_y(1), along_y(-1), along_y(2), OTHER_HI)


def gather(own, ring):
    forward, backward, opposite, other = ring
    to = lambda value, pairs: send(value, pairs)
    across = to(own, other)
    before = to(own, forward)
    behind = to(own, backward)
    far = to(own, opposite)
    across_before = to(across, forward)
    across_behind = to(across, backward)
    across_far = to(far, other)
    return [own, behind, far, before, across, across_behind, across_far, across_before]


def shards(gram, rotations):
    row, col = lax.axis_index("row"), lax.axis_index("col")
    core = col % 2
    from_even = ((core == 0) & (col != 2)) | (col == 15)
    by_relay = (col == 0) | (col == 15)
    keep = lax.dynamic_slice_in_dim(rotations[:, 0], core * N, N, 2)
    give = lax.dynamic_slice_in_dim(rotations[:, 0], (1 - core) * N, N, 2)
    got = send(give, OTHER_CORE)

    def turns(step):
        at = int(step) - 1
        piece = jnp.concatenate([keep[at], got[at]])
        turned = send(piece, TRANSPOSE)
        (half,) = vmem_call(rows_body, gather(piece, ROW_RING), [(2 * N, N)])
        other = send(half, OTHER_CORE)
        (whole,) = vmem_call(join_body, (half, other), [(2 * N, 2 * N)])
        pieces = gather(turned, COL_RING)
        return whole, vmem_call(cols_body, pieces, [(N, N)] * 2)

    def advance(tile, rows, cols):
        own_cols, other_cols = cols
        mixed = mix(rows, tile)
        other = send(mixed, OTHER_CORE)
        own_parts = times(mixed[:N], own_cols), times(mixed[N:], own_cols)
        first, second = lax.optimization_barrier(own_parts)
        first = first + times(other[N:], other_cols)
        second = second + times(other[:N], other_cols)
        first, second = lax.optimization_barrier((first, second))
        end_is_first = ((row == 7) == (core == 0)) & (row != 4)
        ends = jnp.where((row == 3) | end_is_first, first, second)
        first = send(first, MOVE_FIRST)
        ends = send(ends, MOVE_END)
        second = send(second, MOVE_SECOND)
        relayed = send(ends, FROM_RELAY)
        first = jnp.where(by_relay & (row == 4), relayed, first)
        second = jnp.where(by_relay & (row == 3), relayed, second)
        upper = jnp.where(row == 0, ends, jnp.where(from_even, first, second))
        lower = jnp.where(row == 7, ends, jnp.where(from_even, second, first))
        return jnp.concatenate([upper, lower])

    tile = gram
    for step in ("1", "2"):
        tile = advance(tile, *turns(step))
    return tile


def solution(mesh):
    placed = (P("row", "col"), P(None, "row", "col", None))
    return jax.shard_map(
        shards, mesh=mesh, in_specs=placed, out_specs=P("row", "col"), check_vma=False
    )
```

```python
import jax
import jax.numpy as jnp
from jax import lax
from jax.experimental import pallas as pl
from jax.experimental.pallas import tpu as pltpu
from jax.sharding import PartitionSpec as P


N = 512
H = 256
F32 = jnp.float32
HIGH = lax.Precision.HIGH


def place(index):
    row, col = divmod(index, 16)
    return (row // 4, row % 4, col // 8, (col // 2) % 4, col % 2)


def index_of(z_hi, y, z_lo, x, core):
    return (z_hi * 4 + y % 4) * 16 + z_lo * 8 + (x % 4) * 2 + core


def pairs_of(move):
    return [(i, index_of(*move(*place(i)))) for i in range(128)]


def along_x(step):
    return pairs_of(lambda zh, y, zl, x, c: (zh, y, zl, x + step, c))


def along_y(step):
    return pairs_of(lambda zh, y, zl, x, c: (zh, y + step, zl, x, c))


OTHER_LO = pairs_of(lambda zh, y, zl, x, c: (zh, y, 1 - zl, x, c))
OTHER_HI = pairs_of(lambda zh, y, zl, x, c: (1 - zh, y, zl, x, c))
OTHER_CORE = pairs_of(lambda zh, y, zl, x, c: (zh, y, zl, x, 1 - c))
TRANSPOSE = pairs_of(lambda zh, y, zl, x, c: (zl, x, zh, y, c))


def new_position(old):
    if old == 0:
        return 0
    if old == 1:
        return 2
    if old == 14:
        return 15
    return old + 2 if old % 2 == 0 else old - 2


MOVE_COL = [(r * 16 + c, r * 16 + new_position(c)) for r in range(8) for c in range(16)]
ROW_UP = [(r * 16 + c, (r + 1) * 16 + c) for r in range(7) for c in range(16)]
ROW_DOWN = [(r * 16 + c, (r - 1) * 16 + c) for r in range(1, 8) for c in range(16)]


def send(value, pairs):
    return lax.ppermute(value, ("row", "col"), pairs)


def vmem_call(body, inputs, outs):
    return pl.pallas_call(
        body,
        out_shape=[jax.ShapeDtypeStruct(shape, F32) for shape in outs],
        in_specs=[pl.BlockSpec(memory_space=pltpu.VMEM)] * len(inputs),
        out_specs=[pl.BlockSpec(memory_space=pltpu.VMEM)] * len(outs),
        compiler_params=pltpu.CompilerParams(vmem_limit_bytes=12 * 2**20),
        cost_estimate=pl.CostEstimate(flops=0, bytes_accessed=2**22, transcendentals=0),
    )(*inputs)


def rows_body(*refs):
    pieces, out = refs[:4], refs[4]
    col = lax.axis_index("col")
    ring, plane = (col // 2) % 4, col // 8
    for j, piece in enumerate(pieces):
        for part in range(4):
            at = (plane if part < 2 else 1 - plane) * 4 + (ring + j) % 4
            first = at * 128 + 64 * jnp.where(col % 2 == 0, part % 2, 1 - part % 2)
            rows = pl.ds(pl.multiple_of(first, 64), 64)
            out[rows, :] = piece[part * 64 : part * 64 + 64, :]


def join_body(own, other, out):
    up_is_own = (lax.axis_index("col") % 2 == 0) != (lax.axis_index("row") == 0)

    @pl.when(up_is_own)
    def _():
        out[:, 0:N] = own[...]
        out[:, N:] = other[...]

    @pl.when(jnp.logical_not(up_is_own))
    def _():
        out[:, 0:N] = other[...]
        out[:, N:] = own[...]


def cols_body(*refs):
    pieces, own, other = refs[:4], refs[4:6], refs[6:8]
    row, core = lax.axis_index("row"), lax.axis_index("col") % 2
    ring, plane = row % 4, row // 4

    def fill(first, second):
        for j, piece in enumerate(pieces):
            for part in range(4):
                at = (ring + j) % 4 * 128 + 64 * jnp.where(core == 0, part % 2, 1 - part % 2)
                rows = pl.ds(pl.multiple_of(at, 64), 64)
                taken = slice(part * 64, part * 64 + 64)
                for half, out in enumerate(first if part < 2 else second):
                    out[rows, :] = piece[taken, half * H : half * H + H]

    @pl.when(plane == core)
    def _():
        fill(own, other)

    @pl.when(plane != core)
    def _():
        fill(other, own)


def mix(turn, tile):
    dims = (((0,), (0,)), ((), ()))
    return lax.dot_general(turn, tile, dims, precision=HIGH, preferred_element_type=F32)


def times(tile, turn):
    return jnp.dot(tile, turn, precision=HIGH, preferred_element_type=F32)


ROW_RING = (along_x(1), along_x(-1), along_x(2), OTHER_LO)
COL_RING = (along_y(1), along_y(-1), along_y(2), OTHER_HI)


def gather(own, ring):
    forward, backward, opposite, other = ring
    to = lambda value, pairs: send(value, pairs)
    both = jnp.concatenate([own, to(own, other)])
    before = to(both, forward)
    behind = to(both, backward)
    return [both, behind, to(both, opposite), before]


def shards(gram, rotations):
    row = lax.axis_index("row")
    core = lax.axis_index("col") % 2
    keep = lax.dynamic_slice_in_dim(rotations[:, 0], core * N, N, 2)
    give = lax.dynamic_slice_in_dim(rotations[:, 0], (1 - core) * N, N, 2)
    got = send(give, OTHER_CORE)

    def turns(step):
        at = int(step) - 1
        piece = jnp.concatenate([keep[at], got[at]])
        turned = send(piece, TRANSPOSE)
        (half,) = vmem_call(rows_body, gather(piece, ROW_RING), [(2 * N, N)])
        other = send(half, OTHER_CORE)
        (whole,) = vmem_call(join_body, (half, other), [(2 * N, 2 * N)])
        pieces = gather(turned, COL_RING)
        return whole, vmem_call(cols_body, pieces, [(N, H)] * 4)

    def advance(tile, rows, cols):
        own_a, own_b, other_a, other_b = cols
        mixed = mix(rows, tile)
        other = send(mixed, OTHER_CORE)
        own_parts = times(mixed, own_a), times(mixed[:N], own_b), times(mixed[N:], own_b)
        both, up, down = lax.optimization_barrier(own_parts)
        both = both + times(other, other_a)
        up = up + times(other[:N], other_b)
        down = down + times(other[N:], other_b)
        moved = send(both, MOVE_COL)
        row_up = send(up, ROW_UP)
        row_down = send(down, ROW_DOWN)
        moved_up = send(moved[:N], ROW_UP)
        moved_down = send(moved[N:], ROW_DOWN)
        row_up = jnp.where(row == 0, down, row_up)
        row_down = jnp.where(row == 7, up, row_down)
        right = send(jnp.concatenate([row_up, row_down]), MOVE_COL)
        first = jnp.where(row == 0, moved[N:], moved_up)
        second = jnp.where(row == 7, moved[:N], moved_down)
        return jnp.concatenate([jnp.concatenate([first, second]), right], axis=1)

    tile = gram
    for step in ("1", "2"):
        tile = advance(tile, *turns(step))
    return tile


def solution(mesh):
    placed = (P("row", "col"), P(None, "row", "col", None))
    return jax.shard_map(
        shards, mesh=mesh, in_specs=placed, out_specs=P("row", "col"), check_vma=False
    )
```

```python
import jax
import jax.numpy as jnp
from jax import lax
from jax.experimental import pallas as pl
from jax.experimental.pallas import tpu as pltpu
from jax.sharding import PartitionSpec as P


N = 512
H = 256
F32 = jnp.float32
HIGH = lax.Precision.HIGH


def place(index):
    row, col = divmod(index, 16)
    return (row // 4, row % 4, col // 8, (col // 2) % 4, col % 2)


def index_of(z_hi, y, z_lo, x, core):
    return (z_hi * 4 + y % 4) * 16 + z_lo * 8 + (x % 4) * 2 + core


def pairs_of(move):
    return [(i, index_of(*move(*place(i)))) for i in range(128)]


def along_x(step):
    return pairs_of(lambda zh, y, zl, x, c: (zh, y, zl, x + step, c))


def along_y(step):
    return pairs_of(lambda zh, y, zl, x, c: (zh, y + step, zl, x, c))


OTHER_LO = pairs_of(lambda zh, y, zl, x, c: (zh, y, 1 - zl, x, c))
OTHER_HI = pairs_of(lambda zh, y, zl, x, c: (1 - zh, y, zl, x, c))
OTHER_CORE = pairs_of(lambda zh, y, zl, x, c: (zh, y, zl, x, 1 - c))
TRANSPOSE = pairs_of(lambda zh, y, zl, x, c: (zl, x, zh, y, c))


def new_position(old):
    if old == 0:
        return 0
    if old == 1:
        return 2
    if old == 14:
        return 15
    return old + 2 if old % 2 == 0 else old - 2


MOVE_COL = [(r * 16 + c, r * 16 + new_position(c)) for r in range(8) for c in range(16)]
ROW_UP = [(r * 16 + c, (r + 1) * 16 + c) for r in range(7) for c in range(16)]
ROW_DOWN = [(r * 16 + c, (r - 1) * 16 + c) for r in range(1, 8) for c in range(16)]


def send(value, pairs):
    return lax.ppermute(value, ("row", "col"), pairs)


def vmem_call(body, inputs, outs):
    return pl.pallas_call(
        body,
        out_shape=[jax.ShapeDtypeStruct(shape, F32) for shape in outs],
        in_specs=[pl.BlockSpec(memory_space=pltpu.VMEM)] * len(inputs),
        out_specs=[pl.BlockSpec(memory_space=pltpu.VMEM)] * len(outs),
        compiler_params=pltpu.CompilerParams(vmem_limit_bytes=12 * 2**20),
        cost_estimate=pl.CostEstimate(flops=0, bytes_accessed=2**22, transcendentals=0),
    )(*inputs)


def rows_body(*refs):
    pieces, out = refs[:4], refs[4]
    col = lax.axis_index("col")
    ring, plane = (col // 2) % 4, col // 8
    for j, piece in enumerate(pieces):
        for part in range(4):
            at = (plane if part < 2 else 1 - plane) * 4 + (ring + j) % 4
            first = at * 128 + 64 * jnp.where(col % 2 == 0, part % 2, 1 - part % 2)
            rows = pl.ds(pl.multiple_of(first, 64), 64)
            out[rows, :] = piece[part * 64 : part * 64 + 64, :]


def join_body(own, other, out):
    up_is_own = (lax.axis_index("col") % 2 == 0) != (lax.axis_index("row") == 0)

    @pl.when(up_is_own)
    def _():
        out[:, 0:N] = own[...]
        out[:, N:] = other[...]

    @pl.when(jnp.logical_not(up_is_own))
    def _():
        out[:, 0:N] = other[...]
        out[:, N:] = own[...]


def cols_body(*refs):
    pieces, own, other = refs[:-4], refs[-4:-2], refs[-2:]
    row, core = lax.axis_index("row"), lax.axis_index("col") % 2
    ring, plane = row % 4, row // 4

    def fill(first, second):
        for j in range(4):
            for part in range(4):
                at = (ring + j) % 4 * 128 + 64 * jnp.where(core == 0, part % 2, 1 - part % 2)
                rows = pl.ds(pl.multiple_of(at, 64), 64)
                if len(pieces) == 8:
                    piece, begin = pieces[j + part // 2 * 4], part % 2 * 64
                else:
                    piece, begin = pieces[j], part * 64
                for half, out in enumerate(first if part < 2 else second):
                    out[rows, :] = piece[begin : begin + 64, half * H : half * H + H]

    @pl.when(plane == core)
    def _():
        fill(own, other)

    @pl.when(plane != core)
    def _():
        fill(other, own)


def mix(turn, tile):
    dims = (((0,), (0,)), ((), ()))
    return lax.dot_general(turn, tile, dims, precision=HIGH, preferred_element_type=F32)


def times(tile, turn):
    return jnp.dot(tile, turn, precision=HIGH, preferred_element_type=F32)


ROW_RING = (along_x(1), along_x(-1), along_x(2), OTHER_LO)
COL_RING = (along_y(1), along_y(-1), along_y(2), OTHER_HI)


def gather(own, ring, kind, step):
    forward, backward, opposite, other = ring
    to = lambda value, pairs: send(value, pairs)
    across = to(own, other)
    if kind + step != "b1":
        both = jnp.concatenate([own, across])
        before = to(both, forward)
        behind = to(both, backward)
        return [both, behind, to(both, opposite), before]
    before = to(own, forward)
    behind = to(own, backward)
    far = to(own, opposite)
    across_before = to(across, forward)
    across_behind = to(across, backward)
    return [own, behind, far, before, across, across_behind, to(far, other), across_before]


def shards(gram, rotations):
    row = lax.axis_index("row")
    core = lax.axis_index("col") % 2
    keep = lax.dynamic_slice_in_dim(rotations[:, 0], core * N, N, 2)
    give = lax.dynamic_slice_in_dim(rotations[:, 0], (1 - core) * N, N, 2)
    got = send(give, OTHER_CORE)

    def turns(step):
        at = int(step) - 1
        piece = jnp.concatenate([keep[at], got[at]])
        turned = send(piece, TRANSPOSE)
        (half,) = vmem_call(rows_body, gather(piece, ROW_RING, "a", step), [(2 * N, N)])
        other = send(half, OTHER_CORE)
        (whole,) = vmem_call(join_body, (half, other), [(2 * N, 2 * N)])
        pieces = gather(turned, COL_RING, "b", step)
        return whole, vmem_call(cols_body, pieces, [(N, H)] * 4)

    def advance(tile, rows, cols):
        own_a, own_b, other_a, other_b = cols
        mixed = mix(rows, tile)
        other = send(mixed, OTHER_CORE)
        own_parts = times(mixed, own_a), times(mixed[:N], own_b), times(mixed[N:], own_b)
        both, up, down = lax.optimization_barrier(own_parts)
        both = both + times(other, other_a)
        up = up + times(other[:N], other_b)
        down = down + times(other[N:], other_b)
        moved = send(both, MOVE_COL)
        row_up = send(up, ROW_UP)
        row_down = send(down, ROW_DOWN)
        moved_up = send(moved[:N], ROW_UP)
        moved_down = send(moved[N:], ROW_DOWN)
        row_up = jnp.where(row == 0, down, row_up)
        row_down = jnp.where(row == 7, up, row_down)
        right = send(jnp.concatenate([row_up, row_down]), MOVE_COL)
        first = jnp.where(row == 0, moved[N:], moved_up)
        second = jnp.where(row == 7, moved[:N], moved_down)
        return jnp.concatenate([jnp.concatenate([first, second]), right], axis=1)

    tile = gram
    for step in ("1", "2"):
        tile = advance(tile, *turns(step))
    return tile


def solution(mesh):
    placed = (P("row", "col"), P(None, "row", "col", None))
    return jax.shard_map(
        shards, mesh=mesh, in_specs=placed, out_specs=P("row", "col"), check_vma=False
    )
```

```python
import jax
import jax.numpy as jnp
from jax import lax
from jax.experimental import pallas as pl
from jax.experimental.pallas import tpu as pltpu
from jax.sharding import PartitionSpec as P


N = 512
H = 256
F32 = jnp.float32
HIGH = lax.Precision.HIGH


def place(index):
    row, col = divmod(index, 16)
    return (row // 4, row % 4, col // 8, (col // 2) % 4, col % 2)


def index_of(z_hi, y, z_lo, x, core):
    return (z_hi * 4 + y % 4) * 16 + z_lo * 8 + (x % 4) * 2 + core


def pairs_of(move):
    return [(i, index_of(*move(*place(i)))) for i in range(128)]


def along_x(step):
    return pairs_of(lambda zh, y, zl, x, c: (zh, y, zl, x + step, c))


def along_y(step):
    return pairs_of(lambda zh, y, zl, x, c: (zh, y + step, zl, x, c))


OTHER_LO = pairs_of(lambda zh, y, zl, x, c: (zh, y, 1 - zl, x, c))
OTHER_HI = pairs_of(lambda zh, y, zl, x, c: (1 - zh, y, zl, x, c))
OTHER_CORE = pairs_of(lambda zh, y, zl, x, c: (zh, y, zl, x, 1 - c))
TRANSPOSE = pairs_of(lambda zh, y, zl, x, c: (zl, x, zh, y, c))


def new_position(old):
    if old == 0:
        return 0
    if old == 1:
        return 2
    if old == 14:
        return 15
    return old + 2 if old % 2 == 0 else old - 2


MOVE_COL = [(r * 16 + c, r * 16 + new_position(c)) for r in range(8) for c in range(16)]
ROW_UP = [(r * 16 + c, (r + 1) * 16 + c) for r in range(7) for c in range(16)]
ROW_DOWN = [(r * 16 + c, (r - 1) * 16 + c) for r in range(1, 8) for c in range(16)]


def send(value, pairs):
    return lax.ppermute(value, ("row", "col"), pairs)


def vmem_call(body, inputs, outs):
    return pl.pallas_call(
        body,
        out_shape=[jax.ShapeDtypeStruct(shape, F32) for shape in outs],
        in_specs=[pl.BlockSpec(memory_space=pltpu.VMEM)] * len(inputs),
        out_specs=[pl.BlockSpec(memory_space=pltpu.VMEM)] * len(outs),
        compiler_params=pltpu.CompilerParams(vmem_limit_bytes=12 * 2**20),
        cost_estimate=pl.CostEstimate(flops=0, bytes_accessed=2**22, transcendentals=0),
    )(*inputs)


def rows_body(*refs):
    pieces, out = refs[:4], refs[4]
    col = lax.axis_index("col")
    ring, plane = (col // 2) % 4, col // 8
    for j, piece in enumerate(pieces):
        for part in range(4):
            at = (plane if part < 2 else 1 - plane) * 4 + (ring + j) % 4
            first = at * 128 + 64 * jnp.where(col % 2 == 0, part % 2, 1 - part % 2)
            rows = pl.ds(pl.multiple_of(first, 64), 64)
            out[rows, :] = piece[part * 64 : part * 64 + 64, :]


def join_body(own, other, out):
    up_is_own = (lax.axis_index("col") % 2 == 0) != (lax.axis_index("row") == 0)

    @pl.when(up_is_own)
    def _():
        out[:, 0:N] = own[...]
        out[:, N:] = other[...]

    @pl.when(jnp.logical_not(up_is_own))
    def _():
        out[:, 0:N] = other[...]
        out[:, N:] = own[...]


def cols_body(*refs):
    pieces, own, other = refs[:-4], refs[-4:-2], refs[-2:]
    row, core = lax.axis_index("row"), lax.axis_index("col") % 2
    ring, plane = row % 4, row // 4

    def fill(first, second):
        for j in range(4):
            for part in range(4):
                at = (ring + j) % 4 * 128 + 64 * jnp.where(core == 0, part % 2, 1 - part % 2)
                rows = pl.ds(pl.multiple_of(at, 64), 64)
                if len(pieces) == 8:
                    piece, begin = pieces[j + part // 2 * 4], part % 2 * 64
                else:
                    piece, begin = pieces[j], part * 64
                for half, out in enumerate(first if part < 2 else second):
                    out[rows, :] = piece[begin : begin + 64, half * H : half * H + H]

    @pl.when(plane == core)
    def _():
        fill(own, other)

    @pl.when(plane != core)
    def _():
        fill(other, own)


def rows_moved_body(from_above, from_below, up, down, out):
    row = lax.axis_index("row")
    out[0:N, :] = jnp.where(row == 0, down[...], from_above[...])
    out[N:, :] = jnp.where(row == 7, up[...], from_below[...])


def mix(turn, tile):
    dims = (((0,), (0,)), ((), ()))
    return lax.dot_general(turn, tile, dims, precision=HIGH, preferred_element_type=F32)


def times(tile, turn):
    return jnp.dot(tile, turn, precision=HIGH, preferred_element_type=F32)


ROW_RING = (along_x(1), along_x(-1), along_x(2), OTHER_LO)
COL_RING = (along_y(1), along_y(-1), along_y(2), OTHER_HI)


def gather(own, ring, kind, step):
    forward, backward, opposite, other = ring
    to = lambda value, pairs: send(value, pairs)
    across = to(own, other)
    if kind + step != "b1":
        both = jnp.concatenate([own, across])
        before = to(both, forward)
        behind = to(both, backward)
        return [both, behind, to(both, opposite), before]
    before = to(own, forward)
    behind = to(own, backward)
    far = to(own, opposite)
    across_before = to(across, forward)
    across_behind = to(across, backward)
    return [own, behind, far, before, across, across_behind, to(far, other), across_before]


def shards(gram, rotations):
    row = lax.axis_index("row")
    core = lax.axis_index("col") % 2
    keep = lax.dynamic_slice_in_dim(rotations[:, 0], core * N, N, 2)
    give = lax.dynamic_slice_in_dim(rotations[:, 0], (1 - core) * N, N, 2)
    got = send(give, OTHER_CORE)

    def turns(step):
        at = int(step) - 1
        piece = jnp.concatenate([keep[at], got[at]])
        turned = send(piece, TRANSPOSE)
        (half,) = vmem_call(rows_body, gather(piece, ROW_RING, "a", step), [(2 * N, N)])
        other = send(half, OTHER_CORE)
        (whole,) = vmem_call(join_body, (half, other), [(2 * N, 2 * N)])
        pieces = gather(turned, COL_RING, "b", step)
        return whole, vmem_call(cols_body, pieces, [(N, H)] * 4)

    def advance(tile, rows, cols):
        own_a, own_b, other_a, other_b = cols
        mixed = mix(rows, tile)
        other = send(mixed, OTHER_CORE)
        own_parts = times(mixed, own_a), times(mixed[:N], own_b), times(mixed[N:], own_b)
        both, up, down = lax.optimization_barrier(own_parts)
        both = both + times(other, other_a)
        up = up + times(other[:N], other_b)
        down = down + times(other[N:], other_b)
        moved = send(both, MOVE_COL)
        row_up = send(up, ROW_UP)
        row_down = send(down, ROW_DOWN)
        moved_up = send(moved[:N], ROW_UP)
        moved_down = send(moved[N:], ROW_DOWN)
        (right,) = vmem_call(rows_moved_body, (row_up, row_down, up, down), [(2 * N, H)])
        right = send(right, MOVE_COL)
        first = jnp.where(row == 0, moved[N:], moved_up)
        second = jnp.where(row == 7, moved[:N], moved_down)
        return jnp.concatenate([jnp.concatenate([first, second]), right], axis=1)

    tile = gram
    for step in ("1", "2"):
        tile = advance(tile, *turns(step))
    return tile


def solution(mesh):
    placed = (P("row", "col"), P(None, "row", "col", None))
    return jax.shard_map(
        shards, mesh=mesh, in_specs=placed, out_specs=P("row", "col"), check_vma=False
    )
```

```python
import jax
import jax.numpy as jnp
from jax import lax
from jax.experimental import pallas as pl
from jax.experimental.pallas import tpu as pltpu
from jax.sharding import PartitionSpec as P


N = 512
H = 256
F32 = jnp.float32
HIGH = lax.Precision.HIGH


def place(index):
    row, col = divmod(index, 16)
    return (row // 4, row % 4, col // 8, (col // 2) % 4, col % 2)


def index_of(z_hi, y, z_lo, x, core):
    return (z_hi * 4 + y % 4) * 16 + z_lo * 8 + (x % 4) * 2 + core


def pairs_of(move):
    return [(i, index_of(*move(*place(i)))) for i in range(128)]


def along_x(step):
    return pairs_of(lambda zh, y, zl, x, c: (zh, y, zl, x + step, c))


def along_y(step):
    return pairs_of(lambda zh, y, zl, x, c: (zh, y + step, zl, x, c))


OTHER_LO = pairs_of(lambda zh, y, zl, x, c: (zh, y, 1 - zl, x, c))
OTHER_HI = pairs_of(lambda zh, y, zl, x, c: (1 - zh, y, zl, x, c))
OTHER_CORE = pairs_of(lambda zh, y, zl, x, c: (zh, y, zl, x, 1 - c))
TRANSPOSE = pairs_of(lambda zh, y, zl, x, c: (zl, x, zh, y, c))


def new_position(old):
    if old == 0:
        return 0
    if old == 1:
        return 2
    if old == 14:
        return 15
    return old + 2 if old % 2 == 0 else old - 2


MOVE_COL = [(r * 16 + c, r * 16 + new_position(c)) for r in range(8) for c in range(16)]
ROW_UP = [(r * 16 + c, (r + 1) * 16 + c) for r in range(7) for c in range(16)]
ROW_DOWN = [(r * 16 + c, (r - 1) * 16 + c) for r in range(1, 8) for c in range(16)]


def send(value, pairs):
    return lax.ppermute(value, ("row", "col"), pairs)


def vmem_call(body, inputs, outs):
    return pl.pallas_call(
        body,
        out_shape=[jax.ShapeDtypeStruct(shape, F32) for shape in outs],
        in_specs=[pl.BlockSpec(memory_space=pltpu.VMEM)] * len(inputs),
        out_specs=[pl.BlockSpec(memory_space=pltpu.VMEM)] * len(outs),
        compiler_params=pltpu.CompilerParams(vmem_limit_bytes=12 * 2**20),
        cost_estimate=pl.CostEstimate(flops=0, bytes_accessed=2**22, transcendentals=0),
    )(*inputs)


def rows_body(*refs):
    pieces, out = refs[:4], refs[4]
    col = lax.axis_index("col")
    ring, plane = (col // 2) % 4, col // 8
    for j, piece in enumerate(pieces):
        for part in range(4):
            at = (plane if part < 2 else 1 - plane) * 4 + (ring + j) % 4
            first = at * 128 + 64 * jnp.where(col % 2 == 0, part % 2, 1 - part % 2)
            rows = pl.ds(pl.multiple_of(first, 64), 64)
            out[rows, :] = piece[part * 64 : part * 64 + 64, :]


def join_body(own, other, out):
    up_is_own = (lax.axis_index("col") % 2 == 0) != (lax.axis_index("row") == 0)

    @pl.when(up_is_own)
    def _():
        out[:, 0:N] = own[...]
        out[:, N:] = other[...]

    @pl.when(jnp.logical_not(up_is_own))
    def _():
        out[:, 0:N] = other[...]
        out[:, N:] = own[...]


def cols_body(*refs):
    pieces, own, other = refs[:-4], refs[-4:-2], refs[-2:]
    row, core = lax.axis_index("row"), lax.axis_index("col") % 2
    ring, plane = row % 4, row // 4

    def fill(first, second):
        for j in range(4):
            for part in range(4):
                at = (ring + j) % 4 * 128 + 64 * jnp.where(core == 0, part % 2, 1 - part % 2)
                rows = pl.ds(pl.multiple_of(at, 64), 64)
                if len(pieces) == 8:
                    piece, begin = pieces[j + part // 2 * 4], part % 2 * 64
                else:
                    piece, begin = pieces[j], part * 64
                for half, out in enumerate(first if part < 2 else second):
                    out[rows, :] = piece[begin : begin + 64, half * H : half * H + H]

    @pl.when(plane == core)
    def _():
        fill(own, other)

    @pl.when(plane != core)
    def _():
        fill(other, own)


def rows_moved_body(from_above, from_below, up, down, out):
    row = lax.axis_index("row")
    out[0:N, :] = jnp.where(row == 0, down[...], from_above[...])
    out[N:, :] = jnp.where(row == 7, up[...], from_below[...])


def mix(turn, tile):
    dims = (((0,), (0,)), ((), ()))
    return lax.dot_general(turn, tile, dims, precision=HIGH, preferred_element_type=F32)


def times(tile, turn):
    return jnp.dot(tile, turn, precision=HIGH, preferred_element_type=F32)


ROW_RING = (along_x(1), along_x(-1), along_x(2), OTHER_LO)
COL_RING = (along_y(1), along_y(-1), along_y(2), OTHER_HI)


def gather(own, ring, kind, step):
    forward, backward, opposite, other = ring
    to = lambda value, pairs: send(value, pairs)
    across = to(own, other)
    if kind + step != "b1":
        both = jnp.concatenate([own, across])
        before = to(both, forward)
        behind = to(both, backward)
        return [both, behind, to(both, opposite), before]
    before = to(own, forward)
    behind = to(own, backward)
    far = to(own, opposite)
    across_before = to(across, forward)
    across_behind = to(across, backward)
    return [own, behind, far, before, across, across_behind, to(far, other), across_before]


def shards(gram, rotations):
    row = lax.axis_index("row")
    core = lax.axis_index("col") % 2
    keep = lax.dynamic_slice_in_dim(rotations[:, 0], core * N, N, 2)
    give = lax.dynamic_slice_in_dim(rotations[:, 0], (1 - core) * N, N, 2)
    got = send(give, OTHER_CORE)

    def turns(step):
        at = int(step) - 1
        piece = jnp.concatenate([keep[at], got[at]])
        turned = send(piece, TRANSPOSE)
        (half,) = vmem_call(rows_body, gather(piece, ROW_RING, "a", step), [(2 * N, N)])
        other = send(half, OTHER_CORE)
        (whole,) = vmem_call(join_body, (half, other), [(2 * N, 2 * N)])
        pieces = gather(turned, COL_RING, "b", step)
        return whole, vmem_call(cols_body, pieces, [(N, H)] * 4)

    def advance(step, tile, rows, cols):
        own_a, own_b, other_a, other_b = cols
        mixed = mix(rows, tile)
        other = send(mixed, OTHER_CORE)
        own_parts = times(mixed, own_a), times(mixed[:N], own_b), times(mixed[N:], own_b)
        both, up, down = lax.optimization_barrier(own_parts)
        both = both + times(other, other_a)
        up = up + times(other[:N], other_b)
        down = down + times(other[N:], other_b)
        moved = send(both, MOVE_COL)
        row_up = send(up, ROW_UP)
        row_down = send(down, ROW_DOWN)
        moved_up = send(moved[:N], ROW_UP)
        moved_down = send(moved[N:], ROW_DOWN)
        if step == "2":
            (right,) = vmem_call(rows_moved_body, (row_up, row_down, up, down), [(2 * N, H)])
        else:
            row_up = jnp.where(row == 0, down, row_up)
            right = jnp.concatenate([row_up, jnp.where(row == 7, up, row_down)])
        right = send(right, MOVE_COL)
        first = jnp.where(row == 0, moved[N:], moved_up)
        second = jnp.where(row == 7, moved[:N], moved_down)
        return jnp.concatenate([jnp.concatenate([first, second]), right], axis=1)

    tile = gram
    for step in ("1", "2"):
        tile = advance(step, tile, *turns(step))
    return tile


def solution(mesh):
    placed = (P("row", "col"), P(None, "row", "col", None))
    return jax.shard_map(
        shards, mesh=mesh, in_specs=placed, out_specs=P("row", "col"), check_vma=False
    )
```
